256 devices in a mesh: dp: 32 (over x, y, core), group: 8 (over z).
Axes of the slice: x: 4, y: 4, z: 8, core: 2. Of those that a mesh axis runs over, the one named last changes fastest.
Arguments:
- grad_codes: bfloat16 [8, 192, 768, 1024], P('group', None, 'dp'), may hold values from -6 to 6
- row_scales: float32 [8, 192, 768], P('group', None, 'dp'), may hold values from 0.3 to 3
- dither: float32 [8, 192, 768], P('group', None, 'dp'), may hold values from -0.5 to 0.5
- owner_table: int32 [192], replicated, may hold values from 0 to 31, as said below
- matrix_kind: int32 [192], replicated, may hold values from 0 to 1
Outputs:
- updates: bfloat16 [192, 768, 1024], P(None, 'dp', 'group')
- slot_norms: float32 [8, 32, 2], P('group', 'dp')
The draws below stay inside these ranges and needn't reach their ends.
Inputs may be any that keep to these rules, and one draw needn't show every extreme that they name: `owner_table`: within each group of 24 consecutive matrices no owner appears more than 2 times, and in every group some owner appears exactly 2 times. `matrix_kind`: 0 for a gate or up projection, 1 for a down projection stored transposed.
All inputs are finite; a program needn't handle non-finite values.
Results may differ from the reference program's by a relative error of at most 0.018.
Values may be sent and summed in bfloat16 or wider, within the bound.
No kernel may reach another device: no remote copies, remote signals or barrier semaphores. Data moves between devices by JAX's collectives and lax.ppermute only.
A program may use at most 64 MiB of HBM per device.

```python
import math
import jax
import jax.numpy as jnp
from jax import lax

F = 768
D = 1024
ITERS = 2
CAP = 2
MPG = 24
MATS = 192
N_DP = 32
N_GROUP = 8


def draw_owner_table(key, part):
    pieces = []
    for group_index in range(N_GROUP):
        subkey = jax.random.fold_in(key, 101 + group_index)
        first_key, second_key, third_key = jax.random.split(subkey, 3)
        ranking = jax.random.permutation(first_key, N_DP)
        doubled = jnp.minimum(jax.random.randint(second_key, (), 1, 5), MPG // 2)
        position = jnp.arange(MPG)
        picked = jnp.where(position < 2 * doubled, position // 2, position - doubled)
        chosen = ranking[picked]
        shuffle = jax.random.permutation(third_key, MPG)
        pieces.append(chosen[shuffle])
    return jnp.concatenate(pieces).astype(jnp.int32)


def plant(values, key, least, top_value):
    longest = values.shape.index(max(values.shape))
    spots = []
    for shift in (0, 1):
        where = [jax.random.randint(jax.random.fold_in(key, axis), (), 0, length) for axis, length in enumerate(values.shape)]
        where[longest] = (where[longest] + shift) % values.shape[longest]
        spots.append(tuple(where))
    return values.at[spots[0]].set(least).at[spots[1]].set(top_value)


def with_spikes(drawn, key, source, target, shards_of, factor):
    def block_of(dim):
        return (jnp.arange(drawn.shape[dim]) // (drawn.shape[dim] // shards_of)).reshape((-1,) + (1,) * (drawn.ndim - 1 - dim))

    near = jax.random.permutation(key, shards_of)[block_of(target)]
    far = (block_of(target) + shards_of // 2) % shards_of
    return jnp.where((block_of(source) == near) | (block_of(source) == far), factor * drawn, drawn)


def shard_levels(rng, extent, cuts, least, largest):
    loudness = 1.0
    for dim, parts in cuts:
        steps = jax.random.uniform(jax.random.fold_in(jax.random.fold_in(rng, 6), dim), (parts,), jnp.float32, least / len(cuts), largest / len(cuts))
        loudness = loudness * jnp.repeat(jnp.exp(steps), extent[dim] // parts).reshape((-1,) + (1,) * (len(extent) - 1 - dim))
    return loudness


def noise_with(rng, shape, spread, bound, cuts, heavy, kind=jnp.bfloat16):
    drawn = spread * jax.random.normal(rng, shape, jnp.float32)
    if cuts:
        drawn = drawn * shard_levels(rng, shape, cuts, -0.22, 0.18)
    return jnp.clip(with_spikes(drawn, jax.random.fold_in(rng, 3), *heavy), -bound, bound).astype(kind)


def setup_inputs(seed: int = 0) -> dict:
    seeds = jax.random.split(jax.random.key(seed), 6)
    return {
        "grad_codes": noise_with(seeds[0], (N_GROUP, MATS, F, D), 1.0, 6.0, ((0, 8), (2, 32)), (0, 1, 8, 2.0)),
        "row_scales": jnp.clip(jnp.exp(math.log(3.0) - 2.3025851 * jax.random.uniform(seeds[1], (N_GROUP, MATS, F), jnp.float32) ** shard_levels(seeds[1], (N_GROUP, MATS, F), ((0, 8), (2, 32)), -0.2, 0.2)), 0.3, 3.0),
        "dither": jnp.clip(jax.random.uniform(seeds[2], (N_GROUP, MATS, F), jnp.float32, -0.5, 0.5) * shard_levels(seeds[2], (N_GROUP, MATS, F), ((0, 8), (2, 32)), -0.4, 0.0), -0.5, 0.5),
        "owner_table": draw_owner_table(jax.random.fold_in(seeds[5], 71), 0),
        "matrix_kind": plant(jax.random.randint(seeds[4], (MATS,), 0, 2), jax.random.fold_in(seeds[4], 1), 0, 1).astype(jnp.int32),
    }


epsilon = 1e-07
first_coef = 3.4445
second_coef = -4.775
third_coef = 2.0315

def reference(grad_codes, row_scales, dither, owner_table, matrix_kind):
    gate_factor = math.sqrt(max(F, D)) * math.sqrt(max(1.0, F / D))
    down_factor = math.sqrt(max(F, D)) * math.sqrt(max(1.0, D / F))

    def single_matrix(matrix):
        code_block = lax.dynamic_index_in_dim(grad_codes, matrix, 1, keepdims=False)
        scale_rows = lax.dynamic_index_in_dim(row_scales, matrix, 1, keepdims=False)
        dither_rows = lax.dynamic_index_in_dim(dither, matrix, 1, keepdims=False)
        term_block = (scale_rows[:, :, None] * (code_block.astype(jnp.float32) + dither_rows[:, :, None])).astype(jnp.bfloat16)
        term_block = lax.optimization_barrier(term_block)
        grad_sum = lax.optimization_barrier(jnp.sum(term_block.astype(jnp.float32), 0))
        rounded = grad_sum.astype(jnp.bfloat16)
        frob_norm = jnp.sqrt(jnp.sum(jnp.square(rounded.astype(jnp.float32))))
        current = (rounded.astype(jnp.float32) / (frob_norm + epsilon)).astype(jnp.bfloat16)
        for sweep in range(ITERS):
            gram_matrix = jnp.dot(current, current.T, preferred_element_type=jnp.float32).astype(jnp.bfloat16)
            squared = jnp.dot(gram_matrix, gram_matrix, preferred_element_type=jnp.float32)
            polynomial = (second_coef * gram_matrix.astype(jnp.float32) + third_coef * squared).astype(jnp.bfloat16)
            current = (first_coef * current.astype(jnp.float32) + jnp.dot(polynomial, current, preferred_element_type=jnp.float32)).astype(jnp.bfloat16)
        factor = jnp.where(matrix_kind[matrix] == 1, down_factor, gate_factor)
        scaled_update = (current.astype(jnp.float32) * factor).astype(jnp.bfloat16)
        return (scaled_update, frob_norm)
    updates, all_norms = lax.map(single_matrix, jnp.arange(MATS, dtype=jnp.int32))
    owners = owner_table.reshape(N_GROUP, MPG)
    position = jnp.arange(MPG, dtype=jnp.int32)
    same_owner = owners[:, :, None] == owners[:, None, :]
    earlier = position[None, :] < position[:, None]
    slot_of = lax.optimization_barrier(jnp.sum((same_owner & earlier[None]).astype(jnp.int32), -1))
    scaled_norms = all_norms.reshape(N_GROUP, MPG) / math.sqrt(F * D)
    owner_hit = owners[:, :, None] == jnp.arange(N_DP, dtype=jnp.int32)[None, None, :]
    slot_hit = slot_of[:, :, None] == jnp.arange(CAP, dtype=jnp.int32)[None, None, :]
    both_hit = owner_hit[:, :, :, None] & slot_hit[:, :, None, :]
    slot_norms = lax.optimization_barrier(jnp.sum(jnp.where(both_hit, scaled_norms[:, :, None, None], 0.0), 1))
    return (updates, slot_norms)
```

```python
import functools
import math

import jax
import jax.numpy as jnp
from jax import lax
from jax.experimental import pallas as pl
from jax.experimental.pallas import tpu as pltpu
from jax.sharding import PartitionSpec as P

F = 768
D = 1024
ITERS = 2
CAP = 2
STREAMS = 2


epsilon = 1e-07
first_coef = 3.4445
second_coef = -4.775
third_coef = 2.0315


def column_of(table, lane):
    lanes = lax.broadcasted_iota(jnp.int32, table.shape, 1)
    return jnp.sum(jnp.where(lanes == lane, table, 0.0), axis=1, keepdims=True)


def dequantized(codes, scales, shifts, lane):
    return column_of(scales, lane) * (codes.astype(jnp.float32) + column_of(shifts, lane))


def first_kernel(half, targets, up_codes, down_codes, scales_ref, shifts_ref, up_out, down_out):
    per_group = 2 * half
    scales, shifts = scales_ref[...], shifts_ref[...]
    for k in range(half):
        lane = targets[0] * per_group + k
        up_out[k] = dequantized(up_codes[k], scales, shifts, lane).astype(jnp.bfloat16)
        lane = targets[1] * per_group + half + k
        down_out[k] = dequantized(down_codes[k], scales, shifts, lane).astype(jnp.bfloat16)


def second_kernel(
    half,
    targets,
    up_codes,
    down_codes,
    scales_ref,
    shifts_ref,
    up_in,
    down_in,
    up_out,
    down_out,
):
    per_group = 2 * half
    block = pl.program_id(0)
    scales, shifts = scales_ref[...], shifts_ref[...]

    def emit(codes, target, received, out, adding):
        for k in range(half):
            lane = target * per_group + block * half + k
            value = dequantized(codes[k], scales, shifts, lane)
            if adding:
                value = value + received[k].astype(jnp.float32)
            out[k] = value.astype(jnp.bfloat16)

    @pl.when(block == 0)
    def _():
        emit(up_codes, targets[0], up_in, up_out, True)
        emit(down_codes, targets[1], down_in, down_out, False)

    @pl.when(block == 1)
    def _():
        emit(up_codes, targets[0], up_in, up_out, False)
        emit(down_codes, targets[1], down_in, down_out, True)


def later_kernel(
    half,
    targets,
    up_codes,
    down_codes,
    scales_ref,
    shifts_ref,
    up_in,
    down_in,
    up_out,
    down_out,
):
    per_group = 2 * half
    block = pl.program_id(0)
    scales, shifts = scales_ref[...], shifts_ref[...]
    for k in range(half):
        lane = targets[0] * per_group + block * half + k
        value = dequantized(up_codes[k], scales, shifts, lane)
        up_out[k] = (value + up_in[k].astype(jnp.float32)).astype(jnp.bfloat16)
        lane = targets[1] * per_group + block * half + k
        value = dequantized(down_codes[k], scales, shifts, lane)
        down_out[k] = (value + down_in[k].astype(jnp.float32)).astype(jnp.bfloat16)


def last_kernel(count, blocks, targets, codes, scales_ref, shifts_ref, up_in, down_in, out):
    block = pl.program_id(0)
    scales, shifts = scales_ref[...], shifts_ref[...]

    @pl.when(block < blocks)
    def _():
        for k in range(count):
            lane = targets[0] * count * blocks + block * count + k
            value = dequantized(codes[k], scales, shifts, lane)
            value = value + (up_in[k].astype(jnp.float32) + down_in[k].astype(jnp.float32))
            out[k] = value.astype(jnp.bfloat16)

    @pl.when(block >= blocks)
    def _():
        out[...] = jnp.zeros_like(out)


def newton_kernel(
    shard_rows, out_width, factor_ref, *refs
):
    pieces = refs[:STREAMS]
    out_ref, norm_ref, current, gram, poly = refs[STREAMS:]
    height, columns = current.shape
    width = columns // STREAMS
    tile = 8 * shard_rows
    tiles = height // tile
    total = jnp.zeros((1, 1), jnp.float32)
    for stream in range(STREAMS):
        value = pieces[stream][...].astype(jnp.float32)
        total = total + jnp.sum(value * value, keepdims=True)
    norm = jnp.sqrt(total)
    norm_ref[...] = jnp.broadcast_to(norm, norm_ref.shape)
    inverse = 1.0 / (norm + epsilon)
    for stream in range(STREAMS):
        value = pieces[stream][...].astype(jnp.float32)
        current[:, stream * width : (stream + 1) * width] = (value * inverse).astype(jnp.bfloat16)
    for sweep in range(ITERS):
        for i in range(tiles):
            rows = slice(i * tile, (i + 1) * tile)
            product = lax.dot_general(
                current[rows],
                current[...],
                (((1,), (1,)), ((), ())),
                preferred_element_type=jnp.float32,
            )
            gram[rows] = product.astype(jnp.bfloat16)
        for i in range(tiles):
            rows = slice(i * tile, (i + 1) * tile)
            squared = jnp.dot(gram[rows], gram[...], preferred_element_type=jnp.float32)
            poly[rows] = (
                second_coef * gram[rows].astype(jnp.float32) + third_coef * squared
            ).astype(jnp.bfloat16)
        if sweep < ITERS - 1:
            for c in range(columns // 256):
                cols = slice(c * 256, (c + 1) * 256)
                before = current[:, cols]
                product = jnp.dot(poly[...], before, preferred_element_type=jnp.float32)
                current[:, cols] = (
                    first_coef * before.astype(jnp.float32) + product
                ).astype(jnp.bfloat16)
    factor = factor_ref[0]
    per_column = height // shard_rows
    for c in range(columns // 256):
        cols = slice(c * 256, (c + 1) * 256)
        product = jnp.dot(poly[...], current[:, cols], preferred_element_type=jnp.float32)
        result = (first_coef * current[:, cols].astype(jnp.float32) + product).astype(jnp.bfloat16)
        scaled = (result.astype(jnp.float32) * factor).astype(jnp.bfloat16)
        for part in range(256 // out_width):
            first = ((c * 256) // out_width + part) * per_column
            piece = scaled[:, part * out_width : (part + 1) * out_width]
            out_ref[first : first + per_column] = piece.reshape(per_column, shard_rows, out_width)


def on_device(grad_codes, row_scales, dither, owner_table, matrix_kind):
    group_count = lax.axis_size("group")
    owner_count = lax.axis_size("dp")
    matrices = grad_codes.shape[1]
    per_group = matrices // group_count
    shard_rows = grad_codes.shape[2]
    columns = grad_codes.shape[3]
    height = shard_rows * owner_count
    half = per_group // 2
    width = columns // STREAMS
    out_width = columns // group_count
    reach = group_count // 2
    gate_factor = math.sqrt(max(F, D)) * math.sqrt(max(1.0, F / D))
    down_factor = math.sqrt(max(F, D)) * math.sqrt(max(1.0, D / F))
    norm_scale = 1.0 / math.sqrt(height * columns)
    group_index = lax.axis_index("group")
    owner_index = lax.axis_index("dp")
    up = [(i, (i + 1) % group_count) for i in range(group_count)]
    down = [(i, (i - 1) % group_count) for i in range(group_count)]
    codes = grad_codes[0]
    scales = row_scales[0].T
    shifts = dither[0].T
    table = pl.BlockSpec((shard_rows, matrices), lambda i, t: (0, 0))

    def targets_at(distance):
        return jnp.stack(
            [
                lax.rem(group_index + distance, group_count),
                lax.rem(group_index + group_count - distance, group_count),
            ]
        ).astype(jnp.int32)

    def call(kernel, grid, in_specs, out_specs, out_shape, name, operands):
        moved = sum(math.prod(s.shape) * 2 for s in out_shape) * 3
        return pl.pallas_call(
            kernel,
            grid_spec=pltpu.PrefetchScalarGridSpec(
                num_scalar_prefetch=1, grid=grid, in_specs=in_specs, out_specs=out_specs
            ),
            out_shape=out_shape,
            name=name,
            cost_estimate=pl.CostEstimate(flops=0, bytes_accessed=moved, transcendentals=0),
        )(*operands)

    def code_spec(count, blocks, which, first, stream):
        return pl.BlockSpec(
            (count, shard_rows, width), lambda i, t: (t[which] * blocks + first + i, 0, stream)
        )

    block = pl.BlockSpec((half, shard_rows, width), lambda i, t: (i, 0, 0))
    single = pl.BlockSpec((half, shard_rows, width), lambda i, t: (0, 0, 0))
    half_shape = jax.ShapeDtypeStruct((half, shard_rows, width), jnp.bfloat16)
    full_shape = jax.ShapeDtypeStruct((per_group, shard_rows, width), jnp.bfloat16)

    rising = [None] * STREAMS
    falling = [None] * STREAMS
    for step in range(reach):
        distance = reach - step
        targets = targets_at(distance)
        for stream in range(STREAMS):
            if step == 0:
                sends = call(
                    functools.partial(first_kernel, half),
                    (1,),
                    [
                        code_spec(half, 2, 0, 0, stream),
                        code_spec(half, 2, 1, 1, stream),
                        table,
                        table,
                    ],
                    [single, single],
                    [half_shape, half_shape],
                    f"first_{stream}",
                    (targets, codes, codes, scales, shifts),
                )
            else:
                sends = call(
                    functools.partial(second_kernel if step == 1 else later_kernel, half),
                    (2,),
                    [
                        code_spec(half, 2, 0, 0, stream),
                        code_spec(half, 2, 1, 0, stream),
                        table,
                        table,
                        single if step == 1 else block,
                        single if step == 1 else block,
                    ],
                    [block, block],
                    [full_shape, full_shape],
                    f"add_{step}_{stream}",
                    (targets, codes, codes, scales, shifts, rising[stream], falling[stream]),
                )
            rising[stream] = lax.ppermute(sends[0], "group", up)
            falling[stream] = lax.ppermute(sends[1], "group", down)
    pieces = []
    count = math.gcd(per_group, owner_count)
    blocks = per_group // count
    for stream in range(STREAMS):
        received = pl.BlockSpec(
            (count, shard_rows, width), lambda i, t: (jnp.minimum(i, blocks - 1), 0, 0)
        )
        padded = call(
            functools.partial(last_kernel, count, blocks),
            (owner_count // count,),
            [
                pl.BlockSpec(
                    (count, shard_rows, width),
                    lambda i, t: (t[0] * blocks + jnp.minimum(i, blocks - 1), 0, stream),
                ),
                table,
                table,
                received,
                received,
            ],
            [pl.BlockSpec((count, shard_rows, width), lambda i, t: (i, 0, 0))],
            [jax.ShapeDtypeStruct((owner_count, shard_rows, width), jnp.bfloat16)],
            f"last_{stream}",
            (targets_at(0), codes, scales, shifts, rising[stream], falling[stream]),
        )[0]
        arrived = lax.all_to_all(padded, "dp", split_axis=0, concat_axis=0, tiled=True)
        pieces.append(arrived.reshape(height, width))

    owners = lax.dynamic_slice_in_dim(owner_table, group_index * per_group, per_group)
    place = group_index * per_group + jnp.minimum(owner_index, per_group - 1)
    kind = lax.dynamic_slice_in_dim(matrix_kind, place, 1)
    factor = jnp.where(kind == 1, down_factor, gate_factor).astype(jnp.float32)
    whole = pl.BlockSpec(memory_space=pltpu.VMEM)
    blocks_out, norms = pl.pallas_call(
        functools.partial(newton_kernel, shard_rows, out_width),
        in_specs=[pl.BlockSpec(memory_space=pltpu.SMEM)] + [whole] * STREAMS,
        out_specs=[whole, whole],
        out_shape=[
            jax.ShapeDtypeStruct((group_count * owner_count, shard_rows, out_width), jnp.bfloat16),
            jax.ShapeDtypeStruct((8, 128), jnp.float32),
        ],
        scratch_shapes=[
            pltpu.VMEM((height, columns), jnp.bfloat16),
            pltpu.VMEM((height, height), jnp.bfloat16),
            pltpu.VMEM((height, height), jnp.bfloat16),
        ],
        name="newton",
        cost_estimate=pl.CostEstimate(
            flops=2 * ITERS * height * height * (2 * columns + height),
            bytes_accessed=4 * height * columns,
            transcendentals=0,
        ),
        compiler_params=pltpu.CompilerParams(vmem_limit_bytes=40 * 1024 * 1024),
    )(factor, *pieces)
    returned = lax.all_to_all(blocks_out, ("group", "dp"), split_axis=0, concat_axis=0, tiled=True)
    returned = returned.reshape(group_count, owner_count, shard_rows, out_width)
    updates = returned[:, :per_group].reshape(matrices, shard_rows, out_width)

    norms = norms[None]
    stride = 1
    while stride < owner_count:
        partner = [(i, i ^ stride) for i in range(owner_count)]
        other = lax.ppermute(norms, "dp", partner)
        low = (owner_index & stride) == 0
        norms = jnp.concatenate([jnp.where(low, norms, other), jnp.where(low, other, norms)])
        stride *= 2
    all_norms = norms[:per_group, 0, 0]
    position = jnp.arange(per_group, dtype=jnp.int32)
    same_owner = owners[:, None] == owners[None, :]
    earlier = position[None, :] < position[:, None]
    slot_of = jnp.sum((same_owner & earlier).astype(jnp.int32), 1)
    slot_hit = slot_of[:, None] == jnp.arange(CAP, dtype=jnp.int32)[None, :]
    owned_slot = (owners == owner_index)[:, None] & slot_hit
    slot_norms = jnp.sum(jnp.where(owned_slot, all_norms[:, None] * norm_scale, 0.0), 0)
    return (updates, slot_norms.reshape(1, 1, CAP))


def solution(mesh):
    placed = (
        P("group", None, "dp", None),
        P("group", None, "dp"),
        P("group", None, "dp"),
        P(),
        P(),
    )
    return jax.shard_map(
        on_device,
        mesh=mesh,
        in_specs=placed,
        out_specs=(P(None, "dp", "group"), P("group", "dp", None)),
        check_vma=False,
    )
```

```python
import functools
import math

import jax
import jax.numpy as jnp
from jax import lax
from jax.experimental import pallas as pl
from jax.experimental.pallas import tpu as pltpu
from jax.sharding import PartitionSpec as P

F = 768
D = 1024
ITERS = 2
CAP = 2
STREAMS = 2


epsilon = 1e-07
first_coef = 3.4445
second_coef = -4.775
third_coef = 2.0315


def columns_of(table_ref, scratch, target, per_group):
    lanes = table_ref.shape[1]
    scratch[:, :lanes] = table_ref[...]
    wide = scratch.shape[1]
    return pltpu.roll(scratch[...], wide - target * per_group, axis=1)


def dequantized(codes, scales, shifts, k):
    return scales[:, k : k + 1] * (codes.astype(jnp.float32) + shifts[:, k : k + 1])


def hop_kernel(step, half, first_col, targets, codes, scales_ref, shifts_ref, *refs):
    received, (up_out, down_out), scratch = refs[: len(refs) - 5], refs[-5:-3], refs[-3:]
    held, table, sems = scratch
    per_group = 2 * half
    width = held.shape[3]
    parts = ((0, 1), (1, 0)) if step == 0 else ((0, 0), (1, 1), (0, 1), (1, 0))
    copies = []
    for index, (side, part) in enumerate(parts):
        start = targets[side] * per_group + (1 - part if step == 0 else part) * half
        copies.append(
            pltpu.make_async_copy(
                codes.at[pl.ds(start, half), :, pl.ds(first_col, width)],
                held.at[index],
                sems.at[index],
            )
        )
        copies[-1].start()
    tables = [
        [columns_of(ref, table, targets[side], per_group) for ref in (scales_ref, shifts_ref)]
        for side in range(2)
    ]
    for index, (side, part) in enumerate(parts):
        copies[index].wait()
        scales, shifts = tables[side]
        out = (up_out, down_out)[side]
        for k in range(half):
            if step == 0:
                value = dequantized(held[index, k], scales, shifts, (1 - part) * half + k)
                out[k] = value.astype(jnp.bfloat16)
                continue
            value = dequantized(held[index, k], scales, shifts, part * half + k)
            if step > 1:
                value = value + received[side][part * half + k].astype(jnp.float32)
            elif part == side:
                value = value + received[side][k].astype(jnp.float32)
            out[part * half + k] = value.astype(jnp.bfloat16)


def last_kernel(
    half, first_col, targets, codes, scales_ref, shifts_ref, up_in, down_in, out, held, table, sums, sems
):
    per_group = 2 * half
    width = held.shape[3]
    spare = sums.shape[0] - per_group
    copies = []
    for part in range(2):
        copies.append(
            pltpu.make_async_copy(
                codes.at[
                    pl.ds(targets[0] * per_group + part * half, half), :, pl.ds(first_col, width)
                ],
                held.at[part],
                sems.at[part],
            )
        )
        copies[-1].start()
    sums[per_group:] = jnp.zeros((spare,) + sums.shape[1:], sums.dtype)
    scales = columns_of(scales_ref, table, targets[0], per_group)
    shifts = columns_of(shifts_ref, table, targets[0], per_group)
    for part in range(2):
        copies[part].wait()
        for k in range(half):
            place = part * half + k
            value = dequantized(held[part, k], scales, shifts, place)
            value = value + (up_in[place].astype(jnp.float32) + down_in[place].astype(jnp.float32))
            sums[place] = value.astype(jnp.bfloat16)
    store = pltpu.make_async_copy(sums, out, sems.at[2])
    store.start()
    store.wait()


def newton_kernel(
    shard_rows, out_width, factor_ref, *refs
):
    pieces = refs[:STREAMS]
    out_ref, norm_ref, current, gram, poly = refs[STREAMS:]
    height, columns = current.shape
    width = columns // STREAMS
    tile = 8 * shard_rows
    tiles = height // tile
    total = jnp.zeros((1, 1), jnp.float32)
    for stream in range(STREAMS):
        value = pieces[stream][...].astype(jnp.float32)
        total = total + jnp.sum(value * value, keepdims=True)
    norm = jnp.sqrt(total)
    norm_ref[...] = jnp.broadcast_to(norm, norm_ref.shape)
    inverse = 1.0 / (norm + epsilon)
    for stream in range(STREAMS):
        value = pieces[stream][...].astype(jnp.float32)
        current[:, stream * width : (stream + 1) * width] = (value * inverse).astype(jnp.bfloat16)
    for sweep in range(ITERS):
        for i in range(tiles):
            rows = slice(i * tile, (i + 1) * tile)
            product = lax.dot_general(
                current[rows],
                current[...],
                (((1,), (1,)), ((), ())),
                preferred_element_type=jnp.float32,
            )
            gram[rows] = product.astype(jnp.bfloat16)
        for i in range(tiles):
            rows = slice(i * tile, (i + 1) * tile)
            squared = jnp.dot(gram[rows], gram[...], preferred_element_type=jnp.float32)
            poly[rows] = (
                second_coef * gram[rows].astype(jnp.float32) + third_coef * squared
            ).astype(jnp.bfloat16)
        if sweep < ITERS - 1:
            for c in range(columns // 256):
                cols = slice(c * 256, (c + 1) * 256)
                before = current[:, cols]
                product = jnp.dot(poly[...], before, preferred_element_type=jnp.float32)
                current[:, cols] = (
                    first_coef * before.astype(jnp.float32) + product
                ).astype(jnp.bfloat16)
    factor = factor_ref[0]
    per_column = height // shard_rows
    for c in range(columns // 256):
        cols = slice(c * 256, (c + 1) * 256)
        product = jnp.dot(poly[...], current[:, cols], preferred_element_type=jnp.float32)
        result = (first_coef * current[:, cols].astype(jnp.float32) + product).astype(jnp.bfloat16)
        scaled = (result.astype(jnp.float32) * factor).astype(jnp.bfloat16)
        for part in range(256 // out_width):
            first = ((c * 256) // out_width + part) * per_column
            piece = scaled[:, part * out_width : (part + 1) * out_width]
            out_ref[first : first + per_column] = piece.reshape(per_column, shard_rows, out_width)


def program(grad_codes, row_scales, dither, owner_table, matrix_kind):
    group_count = lax.axis_size("group")
    owner_count = lax.axis_size("dp")
    matrices = grad_codes.shape[1]
    per_group = matrices // group_count
    shard_rows = grad_codes.shape[2]
    columns = grad_codes.shape[3]
    height = shard_rows * owner_count
    half = per_group // 2
    width = columns // STREAMS
    out_width = columns // group_count
    reach = group_count // 2
    gate_factor = math.sqrt(max(F, D)) * math.sqrt(max(1.0, F / D))
    down_factor = math.sqrt(max(F, D)) * math.sqrt(max(1.0, D / F))
    norm_scale = 1.0 / math.sqrt(height * columns)
    group_index = lax.axis_index("group")
    owner_index = lax.axis_index("dp")
    up = [(i, (i + 1) % group_count) for i in range(group_count)]
    down = [(i, (i - 1) % group_count) for i in range(group_count)]
    codes = grad_codes[0]
    scales = row_scales[0].T
    shifts = dither[0].T
    whole = pl.BlockSpec(memory_space=pltpu.VMEM)
    anywhere = pl.BlockSpec(memory_space=pl.ANY)
    scalars = pl.BlockSpec(memory_space=pltpu.SMEM)
    table_scratch = pltpu.VMEM((shard_rows, 256), jnp.float32)

    def targets_at(distance):
        return jnp.stack(
            [
                lax.rem(group_index + distance, group_count),
                lax.rem(group_index + group_count - distance, group_count),
            ]
        ).astype(jnp.int32)

    def shape_of(count):
        return jax.ShapeDtypeStruct((count, shard_rows, width), jnp.bfloat16)

    def local(x):
        return pltpu.with_memory_space_constraint(x, pltpu.VMEM)

    def hop(step, stream, targets, received):
        count = half if step == 0 else per_group
        buffers = 2 if step == 0 else 4
        return pl.pallas_call(
            functools.partial(hop_kernel, step, half, stream * width),
            in_specs=[scalars, anywhere, whole, whole] + [whole] * len(received),
            out_specs=[whole, whole],
            out_shape=[pltpu.VMEM(shape_of(count).shape, jnp.bfloat16)] * 2,
            scratch_shapes=[
                pltpu.VMEM((buffers, half, shard_rows, width), jnp.bfloat16),
                table_scratch,
                pltpu.SemaphoreType.DMA((buffers,)),
            ],
            cost_estimate=pl.CostEstimate(
                flops=0, bytes_accessed=6 * count * shard_rows * width, transcendentals=0
            ),
        )(targets, codes, scales, shifts, *[local(x) for x in received])

    def send(blocks):
        rising = lax.ppermute(blocks[0], "group", up)
        falling = lax.ppermute(blocks[1], "group", down)
        return rising, falling

    pending = [()] * STREAMS
    previous = None
    for step in range(reach):
        for stream in range(STREAMS):
            targets = targets_at(reach - step)
            if previous is not None:
                targets, blocks = lax.optimization_barrier((targets, previous[2]))
                pending[previous[1]] = send(blocks)
            previous = (step, stream, hop(step, stream, targets, pending[stream]))
    targets, blocks = lax.optimization_barrier((targets_at(0), previous[2]))
    pending[previous[1]] = send(blocks)
    pieces = []
    for stream in range(STREAMS):
        padded = pl.pallas_call(
            functools.partial(last_kernel, half, stream * width),
            in_specs=[scalars, anywhere, whole, whole, whole, whole],
            out_specs=anywhere,
            out_shape=shape_of(owner_count),
            scratch_shapes=[
                pltpu.VMEM((2, half, shard_rows, width), jnp.bfloat16),
                table_scratch,
                pltpu.VMEM((owner_count, shard_rows, width), jnp.bfloat16),
                pltpu.SemaphoreType.DMA((3,)),
            ],
            cost_estimate=pl.CostEstimate(
                flops=0, bytes_accessed=6 * owner_count * shard_rows * width, transcendentals=0
            ),
        )(targets, codes, scales, shifts, *[local(x) for x in pending[stream]])
        targets, padded = lax.optimization_barrier((targets, padded))
        arrived = lax.all_to_all(padded, "dp", split_axis=0, concat_axis=0, tiled=True)
        pieces.append(arrived.reshape(height, width))

    owners = lax.dynamic_slice_in_dim(owner_table, group_index * per_group, per_group)
    place = group_index * per_group + jnp.minimum(owner_index, per_group - 1)
    kind = lax.dynamic_slice_in_dim(matrix_kind, place, 1)
    factor = jnp.where(kind == 1, down_factor, gate_factor).astype(jnp.float32)
    blocks_out, norms = pl.pallas_call(
        functools.partial(newton_kernel, shard_rows, out_width),
        in_specs=[scalars] + [whole] * STREAMS,
        out_specs=[whole, whole],
        out_shape=[
            jax.ShapeDtypeStruct((group_count * owner_count, shard_rows, out_width), jnp.bfloat16),
            jax.ShapeDtypeStruct((8, 128), jnp.float32),
        ],
        scratch_shapes=[
            pltpu.VMEM((height, columns), jnp.bfloat16),
            pltpu.VMEM((height, height), jnp.bfloat16),
            pltpu.VMEM((height, height), jnp.bfloat16),
        ],
        name="newton",
        cost_estimate=pl.CostEstimate(
            flops=2 * ITERS * height * height * (2 * columns + height),
            bytes_accessed=4 * height * columns,
            transcendentals=0,
        ),
        compiler_params=pltpu.CompilerParams(vmem_limit_bytes=40 * 1024 * 1024),
    )(factor, *pieces)
    returned = lax.all_to_all(blocks_out, ("group", "dp"), split_axis=0, concat_axis=0, tiled=True)
    returned = returned.reshape(group_count, owner_count, shard_rows, out_width)
    updates = returned[:, :per_group].reshape(matrices, shard_rows, out_width)

    norms = norms[None]
    stride = 1
    while stride < owner_count:
        partner = [(i, i ^ stride) for i in range(owner_count)]
        other = lax.ppermute(norms, "dp", partner)
        low = (owner_index & stride) == 0
        norms = jnp.concatenate([jnp.where(low, norms, other), jnp.where(low, other, norms)])
        stride *= 2
    all_norms = norms[:per_group, 0, 0]
    position = jnp.arange(per_group, dtype=jnp.int32)
    same_owner = owners[:, None] == owners[None, :]
    earlier = position[None, :] < position[:, None]
    slot_of = jnp.sum((same_owner & earlier).astype(jnp.int32), 1)
    slot_hit = slot_of[:, None] == jnp.arange(CAP, dtype=jnp.int32)[None, :]
    owned_slot = (owners == owner_index)[:, None] & slot_hit
    slot_norms = jnp.sum(jnp.where(owned_slot, all_norms[:, None] * norm_scale, 0.0), 0)
    return (updates, slot_norms.reshape(1, 1, CAP))


def solution(mesh):
    placed = (
        P("group", None, "dp", None),
        P("group", None, "dp"),
        P("group", None, "dp"),
        P(),
        P(),
    )
    return jax.shard_map(
        program,
        mesh=mesh,
        in_specs=placed,
        out_specs=(P(None, "dp", "group"), P("group", "dp", None)),
        check_vma=False,
    )
```

```python
import functools
import math

import jax
import jax.numpy as jnp
from jax import lax
from jax.experimental import pallas as pl
from jax.experimental.pallas import tpu as pltpu
from jax.sharding import PartitionSpec as P

F = 768
D = 1024
ITERS = 2
CAP = 2
WIDTHS = (384, 640)
STREAMS = len(WIDTHS)
STARTS = tuple(sum(WIDTHS[:stream]) for stream in range(STREAMS))
TILE = 256


epsilon = 1e-07
first_coef = 3.4445
second_coef = -4.775
third_coef = 2.0315


def fetch_tables(tables, kept, sems):
    fetches = [
        pltpu.make_async_copy(table, kept.at[index], sems.at[index])
        for index, table in enumerate(tables)
    ]
    for fetch in fetches:
        fetch.start()
    return fetches


def columns_of(kept, index, scratch, target, per_group):
    lanes = kept.shape[2]
    scratch[:, :lanes] = kept[index]
    wide = scratch.shape[1]
    return pltpu.roll(scratch[...], wide - target * per_group, axis=1)


def dequantized(codes, scales, shifts, k):
    return scales[:, k : k + 1] * (codes.astype(jnp.float32) + shifts[:, k : k + 1])


def hop_kernel(step, half, first_col, groups, codes, scales_ref, shifts_ref, *refs):
    received, (up_out, down_out), scratch = refs[: len(refs) - 9], refs[-9:-7], refs[-7:]
    held, made, kept, table, firsts, loads, stores = scratch
    per_group = 2 * half
    width = held.shape[3]
    here = lax.axis_index("group")
    distance = groups // 2 - step
    targets = (
        lax.rem(here + distance, groups),
        lax.rem(here + groups - distance, groups),
    )
    parts = ((0, 0), (1, 1)) if step == 0 else ((0, 0), (1, 1), (0, 1), (1, 0))
    table_fetches = fetch_tables((scales_ref, shifts_ref), kept, firsts)
    fetches, writes = [], []
    for index, (side, part) in enumerate(parts):
        start = targets[side] * per_group + part * half
        fetches.append(
            pltpu.make_async_copy(
                codes.at[pl.ds(start, half), :, pl.ds(first_col, width)],
                held.at[index],
                loads.at[index],
            )
        )
        fetches[-1].start()
    for fetch in table_fetches:
        fetch.wait()
    tables = [
        [columns_of(kept, index, table, targets[side], per_group) for index in range(2)]
        for side in range(2)
    ]
    for index, (side, part) in enumerate(parts):
        fetches[index].wait()
        scales, shifts = tables[side]
        for k in range(half):
            value = dequantized(held[index, k], scales, shifts, part * half + k)
            if step > 1:
                value = value + received[side][part * half + k].astype(jnp.float32)
            elif step == 1 and part == side:
                value = value + received[side][k].astype(jnp.float32)
            made[index, k] = value.astype(jnp.bfloat16)
        out = (up_out, down_out)[side]
        place = out if step == 0 else out.at[pl.ds(part * half, half)]
        writes.append(pltpu.make_async_copy(made.at[index], place, stores.at[index]))
        writes[-1].start()
    for write in writes:
        write.wait()


def last_kernel(
    half, first_col, codes, scales_ref, shifts_ref, up_in, down_in, out, held, kept, table, sums, firsts, loads, stores
):
    per_group = 2 * half
    width = held.shape[3]
    spare = sums.shape[0] - per_group
    here = lax.axis_index("group")
    table_fetches = fetch_tables((scales_ref, shifts_ref), kept, firsts)
    fetches = []
    for part in range(2):
        fetches.append(
            pltpu.make_async_copy(
                codes.at[pl.ds(here * per_group + part * half, half), :, pl.ds(first_col, width)],
                held.at[part],
                loads.at[part],
            )
        )
        fetches[-1].start()
    sums[per_group:] = jnp.zeros((spare,) + sums.shape[1:], sums.dtype)
    spans = ((per_group, spare), (0, half), (half, half))
    writes = [
        pltpu.make_async_copy(sums.at[pl.ds(*span)], out.at[pl.ds(*span)], stores.at[index])
        for index, span in enumerate(spans)
    ]
    writes[0].start()
    for fetch in table_fetches:
        fetch.wait()
    scales = columns_of(kept, 0, table, here, per_group)
    shifts = columns_of(kept, 1, table, here, per_group)
    for part in range(2):
        fetches[part].wait()
        for k in range(half):
            place = part * half + k
            value = dequantized(held[part, k], scales, shifts, place)
            value = value + (up_in[place].astype(jnp.float32) + down_in[place].astype(jnp.float32))
            sums[place] = value.astype(jnp.bfloat16)
        writes[1 + part].start()
    for write in writes:
        write.wait()


def blocks_of(size):
    return [slice(first, first + TILE) for first in range(0, size, TILE)]


def columns_at(pieces, rows, cols):
    found = []
    for piece, start in zip(pieces, STARTS):
        low = max(cols.start - start, 0)
        high = min(cols.stop - start, piece.shape[1])
        if low < high:
            found.append(piece[rows, low:high])
    return found[0] if len(found) == 1 else jnp.concatenate(found, axis=1)


def newton_kernel(shard_rows, out_width, factor_ref, *refs):
    pieces = refs[:STREAMS]
    out_ref, norm_ref, current, raw, gram, poly, staged, stores = refs[STREAMS:]
    height, columns = current.shape
    row_blocks, col_blocks = blocks_of(height), blocks_of(columns)
    everything = slice(0, height)
    pairs = [(i, j) for i in range(len(row_blocks)) for j in range(i, len(row_blocks))]

    def outer(left, right):
        return lax.dot_general(
            left, right, (((1,), (1,)), ((), ())), preferred_element_type=jnp.float32
        )

    def mirrored(ref, i, j, block):
        ref[row_blocks[i], row_blocks[j]] = block.astype(jnp.bfloat16)
        if i != j:
            ref[row_blocks[j], row_blocks[i]] = block.T.astype(jnp.bfloat16)

    total = jnp.zeros((1, 1), jnp.float32)
    diagonal = lax.broadcasted_iota(jnp.int32, (TILE, TILE), 0) == lax.broadcasted_iota(
        jnp.int32, (TILE, TILE), 1
    )
    span = slice(0, columns)
    for i, j in pairs:
        product = outer(
            columns_at(pieces, row_blocks[i], span), columns_at(pieces, row_blocks[j], span)
        )
        raw[row_blocks[i], row_blocks[j]] = product
        if i == j:
            total = total + jnp.sum(jnp.where(diagonal, product, 0.0), keepdims=True)
    norm = jnp.sqrt(total)
    norm_ref[...] = jnp.broadcast_to(norm, norm_ref.shape)
    inverse = 1.0 / (norm + epsilon)
    for i, j in pairs:
        mirrored(gram, i, j, raw[row_blocks[i], row_blocks[j]] * inverse * inverse)
    writes = []
    for sweep in range(ITERS):
        if sweep > 0:
            for i, j in pairs:
                mirrored(gram, i, j, outer(current[row_blocks[i]], current[row_blocks[j]]))
        for i, j in pairs:
            squared = jnp.dot(
                gram[row_blocks[i]], gram[:, row_blocks[j]], preferred_element_type=jnp.float32
            )
            block = gram[row_blocks[i], row_blocks[j]].astype(jnp.float32)
            mirrored(poly, i, j, second_coef * block + third_coef * squared)
        for index, cols in enumerate(col_blocks):
            before = columns_at(pieces, everything, cols) if sweep == 0 else current[:, cols]
            product = jnp.dot(poly[...], before, preferred_element_type=jnp.float32)
            result = first_coef * before.astype(jnp.float32) + product
            if sweep == 0:
                result = result * inverse
            result = result.astype(jnp.bfloat16)
            if sweep < ITERS - 1:
                current[:, cols] = result
                continue
            scaled = (result.astype(jnp.float32) * factor_ref[0]).astype(jnp.bfloat16)
            per_column = height // shard_rows
            slot = index % 2
            if index >= 2:
                writes[index - 2].wait()
            for part in range(TILE // out_width):
                piece = scaled[:, part * out_width : (part + 1) * out_width]
                staged[slot, part * per_column : (part + 1) * per_column] = piece.reshape(
                    per_column, shard_rows, out_width
                )
            count = TILE // out_width * per_column
            writes.append(
                pltpu.make_async_copy(
                    staged.at[slot], out_ref.at[pl.ds(index * count, count)], stores.at[slot]
                )
            )
            writes[-1].start()
    for write in writes[-2:]:
        write.wait()


def program(grad_codes, row_scales, dither, owner_table, matrix_kind):
    group_count = lax.axis_size("group")
    owner_count = lax.axis_size("dp")
    matrices = grad_codes.shape[1]
    per_group = matrices // group_count
    shard_rows = grad_codes.shape[2]
    columns = grad_codes.shape[3]
    height = shard_rows * owner_count
    half = per_group // 2
    out_width = columns // group_count
    reach = group_count // 2
    gate_factor = math.sqrt(max(F, D)) * math.sqrt(max(1.0, F / D))
    down_factor = math.sqrt(max(F, D)) * math.sqrt(max(1.0, D / F))
    norm_scale = 1.0 / math.sqrt(height * columns)
    group_index = lax.axis_index("group")
    owner_index = lax.axis_index("dp")
    up = [(i, (i + 1) % group_count) for i in range(group_count)]
    down = [(i, (i - 1) % group_count) for i in range(group_count)]
    codes = grad_codes[0]
    scales = row_scales[0].T
    shifts = dither[0].T
    whole = pl.BlockSpec(memory_space=pltpu.VMEM)
    anywhere = pl.BlockSpec(memory_space=pl.ANY)
    scalars = pl.BlockSpec(memory_space=pltpu.SMEM)
    table_scratch = pltpu.VMEM((shard_rows, 256), jnp.float32)

    def shape_of(count, stream):
        return jax.ShapeDtypeStruct((count, shard_rows, WIDTHS[stream]), jnp.bfloat16)

    def buffers_of(count, stream):
        return pltpu.VMEM((count, half, shard_rows, WIDTHS[stream]), jnp.bfloat16)

    def local(x):
        return pltpu.with_memory_space_constraint(x, pltpu.VMEM)

    def cost_of(count, stream):
        moved = 6 * count * shard_rows * WIDTHS[stream]
        return pl.CostEstimate(flops=0, bytes_accessed=moved, transcendentals=0)

    def hop(step, stream, tables, received):
        count = half if step == 0 else per_group
        buffers = 2 if step == 0 else 4
        return pl.pallas_call(
            functools.partial(hop_kernel, step, half, STARTS[stream], group_count),
            in_specs=[anywhere] * 3 + [whole] * len(received),
            out_specs=[anywhere, anywhere],
            out_shape=[shape_of(count, stream)] * 2,
            scratch_shapes=[
                buffers_of(buffers, stream),
                buffers_of(buffers, stream),
                pltpu.VMEM((2, shard_rows, matrices), jnp.float32),
                table_scratch,
                pltpu.SemaphoreType.DMA((2,)),
                pltpu.SemaphoreType.DMA((buffers,)),
                pltpu.SemaphoreType.DMA((buffers,)),
            ],
            cost_estimate=cost_of(count, stream),
        )(codes, *tables, *[local(x) for x in received])

    def send(blocks):
        rising = lax.ppermute(blocks[0], "group", up)
        falling = lax.ppermute(blocks[1], "group", down)
        return rising, falling

    pending = [()] * STREAMS
    tables = (scales, shifts)
    previous = None
    for step in range(reach):
        for stream in range(STREAMS):
            if previous is not None:
                tables, blocks = lax.optimization_barrier((tables, previous[2]))
                pending[previous[1]] = send(blocks)
            previous = (step, stream, hop(step, stream, tables, pending[stream]))
    tables, blocks = lax.optimization_barrier((tables, previous[2]))
    pending[previous[1]] = send(blocks)
    pieces = []
    for stream in range(STREAMS):
        padded = pl.pallas_call(
            functools.partial(last_kernel, half, STARTS[stream]),
            in_specs=[anywhere] * 3 + [whole] * 2,
            out_specs=anywhere,
            out_shape=shape_of(owner_count, stream),
            scratch_shapes=[
                buffers_of(2, stream),
                pltpu.VMEM((2, shard_rows, matrices), jnp.float32),
                table_scratch,
                pltpu.VMEM(shape_of(owner_count, stream).shape, jnp.bfloat16),
                pltpu.SemaphoreType.DMA((2,)),
                pltpu.SemaphoreType.DMA((2,)),
                pltpu.SemaphoreType.DMA((3,)),
            ],
            cost_estimate=cost_of(owner_count, stream),
        )(codes, *tables, *[local(x) for x in pending[stream]])
        tables, padded = lax.optimization_barrier((tables, padded))
        arrived = lax.all_to_all(padded, "dp", split_axis=0, concat_axis=0, tiled=True)
        pieces.append(arrived.reshape(height, WIDTHS[stream]))

    owners = lax.dynamic_slice_in_dim(owner_table, group_index * per_group, per_group)
    place = group_index * per_group + jnp.minimum(owner_index, per_group - 1)
    kind = lax.dynamic_slice_in_dim(matrix_kind, place, 1)
    factor = jnp.where(kind == 1, down_factor, gate_factor).astype(jnp.float32)
    blocks_out, norms = pl.pallas_call(
        functools.partial(newton_kernel, shard_rows, out_width),
        in_specs=[scalars] + [whole] * STREAMS,
        out_specs=[anywhere, whole],
        out_shape=[
            jax.ShapeDtypeStruct((group_count * owner_count, shard_rows, out_width), jnp.bfloat16),
            jax.ShapeDtypeStruct((8, 128), jnp.float32),
        ],
        scratch_shapes=[
            pltpu.VMEM((height, columns), jnp.bfloat16),
            pltpu.VMEM((height, height), jnp.float32),
            pltpu.VMEM((height, height), jnp.bfloat16),
            pltpu.VMEM((height, height), jnp.bfloat16),
            pltpu.VMEM((2, TILE // out_width * owner_count, shard_rows, out_width), jnp.bfloat16),
            pltpu.SemaphoreType.DMA((2,)),
        ],
        name="newton",
        cost_estimate=pl.CostEstimate(
            flops=2 * ITERS * height * height * (2 * columns + height),
            bytes_accessed=4 * height * columns,
            transcendentals=0,
        ),
        compiler_params=pltpu.CompilerParams(vmem_limit_bytes=40 * 1024 * 1024),
    )(factor, *[local(x) for x in pieces])
    returned = lax.all_to_all(blocks_out, ("group", "dp"), split_axis=0, concat_axis=0, tiled=True)
    returned = returned.reshape(group_count, owner_count, shard_rows, out_width)
    updates = returned[:, :per_group].reshape(matrices, shard_rows, out_width)

    norms = norms[None]
    stride = 1
    while stride < owner_count:
        partner = [(i, i ^ stride) for i in range(owner_count)]
        other = lax.ppermute(norms, "dp", partner)
        low = (owner_index & stride) == 0
        norms = jnp.concatenate([jnp.where(low, norms, other), jnp.where(low, other, norms)])
        stride *= 2
    all_norms = norms[:per_group, 0, 0]
    position = jnp.arange(per_group, dtype=jnp.int32)
    same_owner = owners[:, None] == owners[None, :]
    earlier = position[None, :] < position[:, None]
    slot_of = jnp.sum((same_owner & earlier).astype(jnp.int32), 1)
    slot_hit = slot_of[:, None] == jnp.arange(CAP, dtype=jnp.int32)[None, :]
    owned_slot = (owners == owner_index)[:, None] & slot_hit
    slot_norms = jnp.sum(jnp.where(owned_slot, all_norms[:, None] * norm_scale, 0.0), 0)
    return (updates, slot_norms.reshape(1, 1, CAP))


def solution(mesh):
    placed = (
        P("group", None, "dp", None),
        P("group", None, "dp"),
        P("group", None, "dp"),
        P(),
        P(),
    )
    return jax.shard_map(
        program,
        mesh=mesh,
        in_specs=placed,
        out_specs=(P(None, "dp", "group"), P("group", "dp", None)),
        check_vma=False,
    )
```

```python
import functools
import math

import jax
import jax.numpy as jnp
from jax import lax
from jax.experimental import pallas as pl
from jax.experimental.pallas import tpu as pltpu
from jax.sharding import PartitionSpec as P

F = 768
D = 1024
ITERS = 2
CAP = 2
WIDTHS = (384, 640)
STREAMS = len(WIDTHS)
STARTS = tuple(sum(WIDTHS[:stream]) for stream in range(STREAMS))
TILE = 256


epsilon = 1e-07
first_coef = 3.4445
second_coef = -4.775
third_coef = 2.0315


def fetch_tables(tables, kept, sems):
    fetches = [
        pltpu.make_async_copy(table, kept.at[index], sems.at[index])
        for index, table in enumerate(tables)
    ]
    for fetch in fetches:
        fetch.start()
    return fetches


def columns_of(kept, index, scratch, target, per_group):
    lanes = kept.shape[2]
    scratch[:, :lanes] = kept[index]
    wide = scratch.shape[1]
    return pltpu.roll(scratch[...], wide - target * per_group, axis=1)


def dequantized(codes, scales, shifts, k):
    return scales[:, k : k + 1] * (codes.astype(jnp.float32) + shifts[:, k : k + 1])


def hop_kernel(step, half, first_col, groups, codes, scales_ref, shifts_ref, *refs):
    received, (up_out, down_out), scratch = refs[: len(refs) - 9], refs[-9:-7], refs[-7:]
    held, made, kept, table, firsts, loads, stores = scratch
    per_group = 2 * half
    width = held.shape[3]
    here = lax.axis_index("group")
    distance = groups // 2 - step
    targets = (
        lax.rem(here + distance, groups),
        lax.rem(here + groups - distance, groups),
    )
    parts = ((0, 0), (1, 1)) if step == 0 else ((0, 0), (1, 1), (0, 1), (1, 0))
    table_fetches = fetch_tables((scales_ref, shifts_ref), kept, firsts)
    fetches, writes = [], []
    for index, (side, part) in enumerate(parts):
        start = targets[side] * per_group + part * half
        fetches.append(
            pltpu.make_async_copy(
                codes.at[pl.ds(start, half), :, pl.ds(first_col, width)],
                held.at[index],
                loads.at[index],
            )
        )
        fetches[-1].start()
    for fetch in table_fetches:
        fetch.wait()
    tables = [
        [columns_of(kept, index, table, targets[side], per_group) for index in range(2)]
        for side in range(2)
    ]
    for index, (side, part) in enumerate(parts):
        fetches[index].wait()
        scales, shifts = tables[side]
        for k in range(half):
            value = dequantized(held[index, k], scales, shifts, part * half + k)
            if step > 1:
                value = value + received[side][part * half + k].astype(jnp.float32)
            elif step == 1 and part == side:
                value = value + received[side][k].astype(jnp.float32)
            made[index, k] = value.astype(jnp.bfloat16)
        out = (up_out, down_out)[side]
        place = out if step == 0 else out.at[pl.ds(part * half, half)]
        writes.append(pltpu.make_async_copy(made.at[index], place, stores.at[index]))
        writes[-1].start()
    for write in writes:
        write.wait()


def own_kernel(half, first_col, codes, scales_ref, shifts_ref, out, held, kept, table, firsts, loads):
    per_group = 2 * half
    width = held.shape[3]
    here = lax.axis_index("group")
    table_fetches = fetch_tables((scales_ref, shifts_ref), kept, firsts)
    fetches = []
    for part in range(2):
        fetches.append(
            pltpu.make_async_copy(
                codes.at[pl.ds(here * per_group + part * half, half), :, pl.ds(first_col, width)],
                held.at[part],
                loads.at[part],
            )
        )
        fetches[-1].start()
    for fetch in table_fetches:
        fetch.wait()
    scales = columns_of(kept, 0, table, here, per_group)
    shifts = columns_of(kept, 1, table, here, per_group)
    for part in range(2):
        fetches[part].wait()
        for k in range(half):
            value = dequantized(held[part, k], scales, shifts, part * half + k)
            out[part * half + k] = value.astype(jnp.bfloat16)


def last_kernel(own, up_in, down_in, out, sums, stores):
    per_group = own.shape[0]
    spare = sums.shape[0] - per_group
    share = per_group // 4
    sums[per_group:] = jnp.zeros((spare,) + sums.shape[1:], sums.dtype)
    spans = [(per_group, spare)] + [(part * share, share) for part in range(4)]
    writes = [
        pltpu.make_async_copy(sums.at[pl.ds(*span)], out.at[pl.ds(*span)], stores.at[index])
        for index, span in enumerate(spans)
    ]
    writes[0].start()
    for part in range(4):
        for place in range(part * share, (part + 1) * share):
            value = up_in[place].astype(jnp.float32) + down_in[place].astype(jnp.float32)
            sums[place] = (value + own[place].astype(jnp.float32)).astype(jnp.bfloat16)
        writes[1 + part].start()
    for write in writes:
        write.wait()


def blocks_of(size):
    return [slice(first, first + TILE) for first in range(0, size, TILE)]


def columns_at(pieces, rows, cols):
    found = []
    for piece, start in zip(pieces, STARTS):
        low = max(cols.start - start, 0)
        high = min(cols.stop - start, piece.shape[1])
        if low < high:
            found.append(piece[rows, low:high])
    return found[0] if len(found) == 1 else jnp.concatenate(found, axis=1)


def newton_kernel(shard_rows, out_width, factor_ref, *refs):
    pieces = refs[:STREAMS]
    out_ref, norm_ref, current, gram, poly, staged, stores = refs[STREAMS:]
    height, columns = current.shape
    row_blocks, col_blocks = blocks_of(height), blocks_of(columns)
    everything = slice(0, height)
    pairs = [(i, j) for i in range(len(row_blocks)) for j in range(i, len(row_blocks))]

    def outer(left, right):
        return lax.dot_general(
            left, right, (((1,), (1,)), ((), ())), preferred_element_type=jnp.float32
        )

    def mirrored(ref, i, j, block):
        ref[row_blocks[i], row_blocks[j]] = block.astype(jnp.bfloat16)
        if i != j:
            ref[row_blocks[j], row_blocks[i]] = block.T.astype(jnp.bfloat16)

    total = jnp.zeros((1, 1), jnp.float32)
    diagonal = lax.broadcasted_iota(jnp.int32, (TILE, TILE), 0) == lax.broadcasted_iota(
        jnp.int32, (TILE, TILE), 1
    )
    span = slice(0, columns)
    for i, j in pairs:
        product = outer(
            columns_at(pieces, row_blocks[i], span), columns_at(pieces, row_blocks[j], span)
        )
        mirrored(gram, i, j, product)
        if i == j:
            total = total + jnp.sum(jnp.where(diagonal, product, 0.0), keepdims=True)
    norm = jnp.sqrt(total)
    norm_ref[...] = jnp.broadcast_to(norm, norm_ref.shape)
    inverse = 1.0 / (norm + epsilon)
    scale = inverse * inverse
    writes = []
    for sweep in range(ITERS):
        if sweep > 0:
            for i, j in pairs:
                mirrored(gram, i, j, outer(current[row_blocks[i]], current[row_blocks[j]]))
        for i, j in pairs:
            squared = jnp.dot(
                gram[row_blocks[i]], gram[:, row_blocks[j]], preferred_element_type=jnp.float32
            )
            block = gram[row_blocks[i], row_blocks[j]].astype(jnp.float32)
            if sweep == 0:
                block = block * scale
                squared = squared * scale * scale
            mirrored(poly, i, j, second_coef * block + third_coef * squared)
        for index, cols in enumerate(col_blocks):
            before = columns_at(pieces, everything, cols) if sweep == 0 else current[:, cols]
            product = jnp.dot(poly[...], before, preferred_element_type=jnp.float32)
            result = first_coef * before.astype(jnp.float32) + product
            if sweep == 0:
                result = result * inverse
            result = result.astype(jnp.bfloat16)
            if sweep < ITERS - 1:
                current[:, cols] = result
                continue
            scaled = (result.astype(jnp.float32) * factor_ref[0]).astype(jnp.bfloat16)
            per_column = height // shard_rows
            slot = index % 2
            if index >= 2:
                writes[index - 2].wait()
            for part in range(TILE // out_width):
                piece = scaled[:, part * out_width : (part + 1) * out_width]
                staged[slot, part * per_column : (part + 1) * per_column] = piece.reshape(
                    per_column, shard_rows, out_width
                )
            count = TILE // out_width * per_column
            writes.append(
                pltpu.make_async_copy(
                    staged.at[slot], out_ref.at[pl.ds(index * count, count)], stores.at[slot]
                )
            )
            writes[-1].start()
    for write in writes[-2:]:
        write.wait()


def program(grad_codes, row_scales, dither, owner_table, matrix_kind):
    group_count = lax.axis_size("group")
    owner_count = lax.axis_size("dp")
    matrices = grad_codes.shape[1]
    per_group = matrices // group_count
    shard_rows = grad_codes.shape[2]
    columns = grad_codes.shape[3]
    height = shard_rows * owner_count
    half = per_group // 2
    out_width = columns // group_count
    reach = group_count // 2
    gate_factor = math.sqrt(max(F, D)) * math.sqrt(max(1.0, F / D))
    down_factor = math.sqrt(max(F, D)) * math.sqrt(max(1.0, D / F))
    norm_scale = 1.0 / math.sqrt(height * columns)
    group_index = lax.axis_index("group")
    owner_index = lax.axis_index("dp")
    up = [(i, (i + 1) % group_count) for i in range(group_count)]
    down = [(i, (i - 1) % group_count) for i in range(group_count)]
    codes = grad_codes[0]
    scales = row_scales[0].T
    shifts = dither[0].T
    whole = pl.BlockSpec(memory_space=pltpu.VMEM)
    anywhere = pl.BlockSpec(memory_space=pl.ANY)
    outside = pl.BlockSpec(memory_space=pltpu.HBM)
    scalars = pl.BlockSpec(memory_space=pltpu.SMEM)
    table_scratch = pltpu.VMEM((shard_rows, 256), jnp.float32)

    lean = pltpu.CompilerParams(vmem_limit_bytes=10 * 1024 * 1024)

    def shape_of(count, stream):
        return jax.ShapeDtypeStruct((count, shard_rows, WIDTHS[stream]), jnp.bfloat16)

    def buffers_of(count, stream):
        return pltpu.VMEM((count, half, shard_rows, WIDTHS[stream]), jnp.bfloat16)

    def local(x):
        return pltpu.with_memory_space_constraint(x, pltpu.VMEM)

    def cost_of(count, stream):
        moved = 6 * count * shard_rows * WIDTHS[stream]
        return pl.CostEstimate(flops=0, bytes_accessed=moved, transcendentals=0)

    def remote(x):
        return pltpu.with_memory_space_constraint(x, pltpu.HBM)

    def hop(step, stream, tables, received):
        count = half if step == 0 else per_group
        buffers = 2 if step == 0 else 4
        return pl.pallas_call(
            functools.partial(hop_kernel, step, half, STARTS[stream], group_count),
            in_specs=[outside] * 3 + [whole] * len(received),
            out_specs=[anywhere, anywhere],
            out_shape=[shape_of(count, stream)] * 2,
            scratch_shapes=[
                buffers_of(buffers, stream),
                buffers_of(buffers, stream),
                pltpu.VMEM((2, shard_rows, matrices), jnp.float32),
                table_scratch,
                pltpu.SemaphoreType.DMA((2,)),
                pltpu.SemaphoreType.DMA((buffers,)),
                pltpu.SemaphoreType.DMA((buffers,)),
            ],
            cost_estimate=cost_of(count, stream),
            compiler_params=lean,
        )(remote(codes), *[remote(x) for x in tables], *[local(x) for x in received])

    def send(blocks):
        rising = lax.ppermute(blocks[0], "group", up)
        falling = lax.ppermute(blocks[1], "group", down)
        return rising, falling

    def own(stream, tables):
        return pl.pallas_call(
            functools.partial(own_kernel, half, STARTS[stream]),
            in_specs=[outside] * 3,
            out_specs=whole,
            out_shape=shape_of(per_group, stream),
            scratch_shapes=[
                buffers_of(2, stream),
                pltpu.VMEM((2, shard_rows, matrices), jnp.float32),
                table_scratch,
                pltpu.SemaphoreType.DMA((2,)),
                pltpu.SemaphoreType.DMA((2,)),
            ],
            cost_estimate=cost_of(per_group, stream),
            compiler_params=lean,
        )(remote(codes), *[remote(x) for x in tables])

    owns = []
    pending = [()] * STREAMS
    tables = (scales, shifts)
    previous = None
    for step in range(reach):
        for stream in range(STREAMS):
            if previous is not None:
                tables, blocks = lax.optimization_barrier((tables, previous[2]))
                pending[previous[1]] = send(blocks)
            if (step, stream) == (reach - 1, STREAMS - 1):
                for each in range(STREAMS):
                    owns.append(own(each, tables))
                    tables, owns[each] = lax.optimization_barrier((tables, owns[each]))
            previous = (step, stream, hop(step, stream, tables, pending[stream]))
    owns, blocks = lax.optimization_barrier((owns, previous[2]))
    pending[previous[1]] = send(blocks)
    pieces = []
    for stream in range(STREAMS):
        padded = pl.pallas_call(
            last_kernel,
            in_specs=[whole] * 3,
            out_specs=anywhere,
            out_shape=shape_of(owner_count, stream),
            scratch_shapes=[
                pltpu.VMEM(shape_of(owner_count, stream).shape, jnp.bfloat16),
                pltpu.SemaphoreType.DMA((5,)),
            ],
            cost_estimate=cost_of(owner_count, stream),
            compiler_params=lean,
        )(local(owns[stream]), *[local(x) for x in pending[stream]])
        owns, padded = lax.optimization_barrier((owns, padded))
        arrived = lax.all_to_all(padded, "dp", split_axis=0, concat_axis=0, tiled=True)
        pieces.append(arrived.reshape(height, WIDTHS[stream]))

    owners = lax.dynamic_slice_in_dim(owner_table, group_index * per_group, per_group)
    place = group_index * per_group + jnp.minimum(owner_index, per_group - 1)
    kind = lax.dynamic_slice_in_dim(matrix_kind, place, 1)
    factor = jnp.where(kind == 1, down_factor, gate_factor).astype(jnp.float32)
    blocks_out, norms = pl.pallas_call(
        functools.partial(newton_kernel, shard_rows, out_width),
        in_specs=[scalars] + [whole] * STREAMS,
        out_specs=[anywhere, whole],
        out_shape=[
            jax.ShapeDtypeStruct((group_count * owner_count, shard_rows, out_width), jnp.bfloat16),
            jax.ShapeDtypeStruct((8, 128), jnp.float32),
        ],
        scratch_shapes=[
            pltpu.VMEM((height, columns), jnp.bfloat16),
            pltpu.VMEM((height, height), jnp.bfloat16),
            pltpu.VMEM((height, height), jnp.bfloat16),
            pltpu.VMEM((2, TILE // out_width * owner_count, shard_rows, out_width), jnp.bfloat16),
            pltpu.SemaphoreType.DMA((2,)),
        ],
        name="newton",
        cost_estimate=pl.CostEstimate(
            flops=2 * ITERS * height * height * (2 * columns + height),
            bytes_accessed=4 * height * columns,
            transcendentals=0,
        ),
        compiler_params=pltpu.CompilerParams(vmem_limit_bytes=20 * 1024 * 1024),
    )(factor, *[local(x) for x in pieces])
    returned = lax.all_to_all(blocks_out, ("group", "dp"), split_axis=0, concat_axis=0, tiled=True)
    returned = returned.reshape(group_count, owner_count, shard_rows, out_width)
    updates = returned[:, :per_group].reshape(matrices, shard_rows, out_width)

    norms = norms[None]
    stride = 1
    while stride < owner_count:
        partner = [(i, i ^ stride) for i in range(owner_count)]
        other = lax.ppermute(norms, "dp", partner)
        low = (owner_index & stride) == 0
        norms = jnp.concatenate([jnp.where(low, norms, other), jnp.where(low, other, norms)])
        stride *= 2
    all_norms = norms[:per_group, 0, 0]
    position = jnp.arange(per_group, dtype=jnp.int32)
    same_owner = owners[:, None] == owners[None, :]
    earlier = position[None, :] < position[:, None]
    slot_of = jnp.sum((same_owner & earlier).astype(jnp.int32), 1)
    slot_hit = slot_of[:, None] == jnp.arange(CAP, dtype=jnp.int32)[None, :]
    owned_slot = (owners == owner_index)[:, None] & slot_hit
    slot_norms = jnp.sum(jnp.where(owned_slot, all_norms[:, None] * norm_scale, 0.0), 0)
    return (updates, slot_norms.reshape(1, 1, CAP))


def solution(mesh):
    placed = (
        P("group", None, "dp", None),
        P("group", None, "dp"),
        P("group", None, "dp"),
        P(),
        P(),
    )
    return jax.shard_map(
        program,
        mesh=mesh,
        in_specs=placed,
        out_specs=(P(None, "dp", "group"), P("group", "dp", None)),
        check_vma=False,
    )
```
